768 devices in a mesh: inter: 24 (over z, y_hi), intra: 32 (over y_lo, x, core).
Axes of the slice: x: 4, y: 8 (y_hi: 2, y_lo: 4; y = y_hi * 4 + y_lo), z: 12, core: 2. Of those that a mesh axis runs over, the one named last changes fastest.
Arguments:
- tokens: bfloat16 [98304, 8192], P(('inter', 'intra'))
- flat_params: bfloat16 [1056768], P(('inter', 'intra'))
- cotangent: bfloat16 [98304, 128], P(('inter', 'intra')), may hold values from -6 to 6
Outputs:
- values: bfloat16 [98304, 128], P(('inter', 'intra'))
- token_grads: bfloat16 [98304, 8192], P(('inter', 'intra'))
- param_grads: float32 [1056768], P(('inter', 'intra'))
The draws below stay inside these ranges and needn't reach their ends.
All inputs are finite; a program needn't handle non-finite values.
Results may differ from the reference program's by a relative error of at most 0.0049.
Values may be sent and summed in bfloat16 or wider, within the bound.
No kernel may reach another device: no remote copies, remote signals or barrier semaphores. Data moves between devices by JAX's collectives and lax.ppermute only.
A program may use at most 64 MiB of HBM per device.

```python
import math
import jax
import jax.numpy as jnp
from jax import lax

D = 8192
HEAD = 128
TOK_DEV = 128
TOKENS = 98304


def draw_tokens(key, part):
    keys = jax.random.split(jax.random.fold_in(key, 11), 4)
    normal_part = jnp.clip(jax.random.normal(keys[0], (TOKENS, D), jnp.float32), -4.0, 4.0)
    row_scale = jnp.exp(jax.random.uniform(keys[1], (TOKENS, 1), jnp.float32, jnp.log(0.3), jnp.log(3.0)))
    col_scale = jnp.exp(jax.random.uniform(keys[2], (1, D), jnp.float32, jnp.log(0.5), jnp.log(5.0)))
    count_blocks = TOKENS // TOK_DEV
    permuted = jax.random.permutation(keys[3], count_blocks)
    token_block = permuted[jnp.arange(TOKENS) // TOK_DEV]
    column_block = jnp.arange(D) * count_blocks // D
    spiked = jnp.where(token_block[:, None] == column_block[None, :], 4.0, 1.0)
    return (normal_part * row_scale * col_scale * spiked).astype(jnp.bfloat16)


def draw_flat_params(key, part):
    keys = jax.random.split(jax.random.fold_in(key, 23), 2)
    gains = jax.random.uniform(keys[0], (D,), jnp.float32, 0.5, 1.5)
    weights = jnp.clip(jax.random.normal(keys[1], (D * HEAD,), jnp.float32), -4.0, 4.0)
    weights = weights * D ** (-0.5)
    return jnp.concatenate([gains, weights]).astype(jnp.bfloat16)


def block_levels(own_key, dims, shards, least, high):
    level, own = 1.0, jax.random.fold_in(own_key, 6)
    for axis_at, shards_of in shards:
        steps = jnp.exp(jax.random.uniform(jax.random.fold_in(own, axis_at), (shards_of,), jnp.float32, least / len(shards), high / len(shards)))
        level = level * jnp.repeat(steps, dims[axis_at] // shards_of).reshape([-1 if axis == axis_at else 1 for axis in range(len(dims))])
    return level


def bell_draw(key, extent, deviation, most, cuts=(), kind=jnp.bfloat16):
    entries = jax.random.normal(key, extent, jnp.float32) * deviation
    if len(cuts) > 0:
        entries = block_levels(key, extent, cuts, -0.22, 0.18) * entries
    return jnp.clip(entries, min=-most, max=most).astype(kind)


def setup_inputs(seed: int = 0) -> dict:
    arg_keys = jax.random.split(jax.random.key(seed), 4)
    tokens = draw_tokens(jax.random.fold_in(arg_keys[3], 71), 0)
    flat_params = draw_flat_params(jax.random.fold_in(arg_keys[3], 71), 0)
    cotangent = bell_draw(arg_keys[2], (TOKENS, HEAD), 1.0, 6.0, ((0, 768),))
    return {"tokens": tokens, "flat_params": flat_params, "cotangent": cotangent}


def reference(tokens, flat_params, cotangent):
    gain = flat_params[:D].astype(jnp.float32)
    weight = flat_params[D:].reshape(D, HEAD)
    block_rows = math.gcd(TOKENS, 4096)
    blocks = TOKENS // block_rows
    token_blocks = tokens.reshape(blocks, block_rows, D)
    cot_blocks = cotangent.reshape(blocks, block_rows, HEAD)

    def advance(totals, inputs_pair):
        token_part, cot_part = inputs_pair
        as_float = token_part.astype(jnp.float32)
        inverse = lax.rsqrt(lax.optimization_barrier(jnp.mean(as_float * as_float, axis=1, keepdims=True)) + 1e-05)
        normed = as_float * inverse
        hidden = (normed * gain).astype(jnp.bfloat16)
        values = jnp.dot(hidden, weight, preferred_element_type=jnp.float32).astype(jnp.bfloat16)
        hidden_grad = jnp.dot(cot_part, weight.T, preferred_element_type=jnp.float32)
        gain_part = lax.optimization_barrier(jnp.sum(hidden_grad * normed, axis=0))
        weight_part = jnp.dot(hidden.T, cot_part, preferred_element_type=jnp.float32)
        normed_grad = hidden_grad * gain
        token_grads = inverse * (normed_grad - normed * lax.optimization_barrier(jnp.mean(normed_grad * normed, axis=1, keepdims=True)))
        return ((totals[0] + gain_part, totals[1] + weight_part), (values, token_grads.astype(jnp.bfloat16)))
    start = (jnp.zeros((D,), jnp.float32), jnp.zeros((D, HEAD), jnp.float32))
    (gain_grad, weight_grad), (values, token_grads) = lax.scan(advance, start, (token_blocks, cot_blocks))
    param_grads = jnp.concatenate([gain_grad, weight_grad.reshape(-1)])
    return (values.reshape(TOKENS, HEAD), token_grads.reshape(TOKENS, D), param_grads)
```

```python
import jax
import jax.numpy as jnp
from jax import lax
from jax.experimental import pallas as pl
from jax.experimental.pallas import tpu as pltpu
from jax.sharding import Mesh, PartitionSpec as P

NZ, NYH, NYL, NX, NC = 12, 2, 4, 4, 2
NY = NYH * NYL
Y = ("yh", "yl")
ALL = ("z", "yh", "yl", "x", "c")
LANES = 128
ROWS = 12
GROUP = 43
OFFS = (0, 10, 21, 32)
SPAN = 24
STEPS = NZ // 2
BLOCKS = NC * NX * NY
CHUNK = 512


def pieces():
    for zl in range(2):
        for y in range(NY):
            for a in range(NX // 2):
                src = []
                for j in range(4):
                    block = ((j & 1) * NX + 2 * a + (j >> 1)) * NY + y
                    src.append(block * SPAN + ROWS * zl)
                yield 2 * GROUP * NY * zl + 2 * GROUP * y + GROUP * a, src


STEP_ROWS = 2 * 2 * GROUP * NY


def kernel(tok_ref, gw_ref, cot_ref, val_ref, tg_ref, pg_ref, w_ref, st_ref, p_ref, h_ref):
    rows, width = tok_ref.shape
    gain_rows = width // LANES
    zone = NZ * ROWS

    def assemble(zz, _):
        for s in range(BLOCKS):
            start = pl.multiple_of(s * zone + zz * SPAN, 8)
            st_ref[s * SPAN : (s + 1) * SPAN, :] = gw_ref[pl.ds(start, SPAN), :].astype(jnp.float32)
        out = w_ref.at[pl.ds(pl.multiple_of(zz * STEP_ROWS, 8), STEP_ROWS)]
        for base, src in pieces():
            for j in range(4):
                lo = 0 if j == 0 else 1
                t = src[j]
                out[base + OFFS[j] + lo : base + OFFS[j] + lo + 10, :] = st_ref[t + lo : t + lo + 10, :]
                if j < 3:
                    at = 10 if j == 0 else 11
                    out[base + OFFS[j + 1] : base + OFFS[j + 1] + 1, :] = (
                        st_ref[t + at : t + at + 1, :] + st_ref[src[j + 1] : src[j + 1] + 1, :]
                    )
        return 0

    lax.fori_loop(0, STEPS, assemble, 0)

    def fold(v):
        total = v[:, :LANES]
        for i in range(1, CHUNK // LANES):
            total = total + v[:, i * LANES : (i + 1) * LANES]
        return total

    def cols(k):
        return pl.ds(pl.multiple_of(k * CHUNK, CHUNK), CHUNK)

    def squares(k, acc):
        x = tok_ref[:, cols(k)].astype(jnp.float32)
        return acc + fold(x * x)

    steps = width // CHUNK
    zero = jnp.zeros((rows, LANES), jnp.float32)
    acc = lax.fori_loop(0, steps, squares, zero)
    inverse = lax.rsqrt(jnp.sum(acc, axis=1, keepdims=True) * (1.0 / width) + 1e-05)
    per = CHUNK // LANES
    cot = cot_ref[...]
    p_ref[gain_rows + width :, :] = jnp.zeros((8, LANES), jnp.float32)

    def main(k, carry):
        values, dots = carry
        normed = tok_ref[:, cols(k)].astype(jnp.float32) * inverse
        gain = jnp.concatenate([w_ref[pl.ds(k * per + i, 1), :] for i in range(per)], axis=1)
        at = pl.ds(pl.multiple_of(gain_rows + k * CHUNK, 8), CHUNK)
        weight = w_ref[at, :].astype(jnp.bfloat16)
        hidden = (normed * gain).astype(jnp.bfloat16)
        values = values + jnp.dot(hidden, weight, preferred_element_type=jnp.float32)
        p_ref[at, :] = lax.dot_general(
            hidden, cot, (((0,), (0,)), ((), ())), preferred_element_type=jnp.float32
        )
        hidden_grad = lax.dot_general(
            cot, weight, (((1,), (1,)), ((), ())), preferred_element_type=jnp.float32
        )
        gain_grad = jnp.sum(hidden_grad * normed, axis=0, keepdims=True)
        for i in range(per):
            p_ref[pl.ds(k * per + i, 1), :] = gain_grad[:, i * LANES : (i + 1) * LANES]
        normed_grad = hidden_grad * gain
        h_ref[:, cols(k)] = normed_grad
        return values, dots + fold(normed_grad * normed)

    values, dots = lax.fori_loop(0, steps, main, (zero, zero))
    val_ref[...] = values.astype(val_ref.dtype)
    mean = jnp.sum(dots, axis=1, keepdims=True) * (1.0 / width)

    def finish(k, _):
        normed = tok_ref[:, cols(k)].astype(jnp.float32) * inverse
        tg_ref[:, cols(k)] = (inverse * (h_ref[:, cols(k)] - normed * mean)).astype(tg_ref.dtype)
        return 0

    lax.fori_loop(0, steps, finish, 0)

    def split(zz, _):
        src_rows = p_ref.at[pl.ds(pl.multiple_of(zz * STEP_ROWS, 8), STEP_ROWS + 8)]
        for base, dst in pieces():
            for j in range(4):
                r = base + OFFS[j]
                st_ref[dst[j] : dst[j] + ROWS, :] = src_rows[r : r + ROWS, :]
        for s in range(BLOCKS):
            start = pl.multiple_of(s * zone + zz * SPAN, 8)
            pg_ref[pl.ds(start, SPAN), :] = st_ref[s * SPAN : (s + 1) * SPAN, :].astype(pg_ref.dtype)
        return 0

    lax.fori_loop(0, STEPS, split, 0)


def local_step(tokens, gathered, cotangent):
    rows, width = tokens.shape
    total = width // LANES + width
    vmem = pl.BlockSpec(memory_space=pltpu.VMEM)
    return pl.pallas_call(
        kernel,
        out_shape=(
            jax.ShapeDtypeStruct(cotangent.shape, jnp.bfloat16),
            jax.ShapeDtypeStruct(tokens.shape, jnp.bfloat16),
            jax.ShapeDtypeStruct(gathered.shape, jnp.bfloat16),
        ),
        in_specs=[vmem] * 3,
        out_specs=[vmem] * 3,
        scratch_shapes=[
            pltpu.VMEM((total, LANES), jnp.float32),
            pltpu.VMEM((BLOCKS * SPAN, LANES), jnp.float32),
            pltpu.VMEM((total + 8, LANES), jnp.float32),
            pltpu.VMEM((rows, width), jnp.float32),
        ],
        compiler_params=pltpu.CompilerParams(vmem_limit_bytes=48 * 1024 * 1024),
        name="local_step",
    )(tokens, gathered, cotangent)


def spread(piece, axis, count):
    return lax.all_to_all(
        jnp.broadcast_to(piece[None], (count,) + piece.shape), axis, 0, 0, tiled=True
    )


def collect(parts, axis, dtype):
    got = lax.all_to_all(parts.astype(dtype), axis, 0, 0, tiled=True)
    return jnp.sum(got.astype(jnp.float32), axis=0)


def phase():
    j = (lax.axis_index("x") % 2) * 2 + lax.axis_index("c")
    return (j * 96) % LANES


def on_device(tokens, flat_params, cotangent):
    shard_len = flat_params.shape[0]
    offset = phase()
    piece = lax.dynamic_update_slice(
        jnp.zeros((ROWS * LANES,), flat_params.dtype), flat_params, (offset,)
    ).reshape(ROWS, LANES)
    piece = spread(piece, "z", NZ).reshape(NZ * ROWS, LANES)
    piece = spread(piece, Y, NY).reshape(NY * NZ * ROWS, LANES)
    piece = spread(piece, "x", NX).reshape(NX * NY * NZ * ROWS, LANES)
    piece = spread(piece, "c", NC).reshape(BLOCKS * NZ * ROWS, LANES)
    values, token_grads, grads = local_step(tokens, piece, cotangent)
    grads = collect(grads.reshape(NC, -1, LANES), "c", jnp.bfloat16)
    grads = collect(grads.reshape(NX, -1, LANES), "x", jnp.bfloat16)
    grads = collect(grads.reshape(NY, -1, LANES), Y, jnp.bfloat16)
    grads = collect(grads.reshape(NZ, ROWS, LANES), "z", jnp.float32)
    owned = lax.dynamic_slice(grads.reshape(-1), (offset,), (shard_len,))
    return values, token_grads, owned


def solution(mesh):
    split = Mesh(mesh.devices.reshape(NZ, NYH, NYL, NX, NC), ALL)
    specs = (P(ALL, None), P(ALL), P(ALL, None))
    return jax.shard_map(
        on_device,
        mesh=split,
        in_specs=specs,
        out_specs=(P(ALL, None), P(ALL, None), P(ALL)),
        check_vma=False,
    )
```

```python
import jax
import jax.numpy as jnp
from jax import lax
from jax.experimental import pallas as pl
from jax.experimental.pallas import tpu as pltpu
from jax.sharding import Mesh, PartitionSpec as P

NZ, NYH, NYL, NX, NC = 12, 2, 4, 4, 2
NY = NYH * NYL
Y = ("yh", "yl")
ALL = ("z", "yh", "yl", "x", "c")
LANES = 128
ROWS = 12
GROUP = 43
OFFS = (0, 10, 21, 32)
SPAN = 24
STEPS = NZ // 2
BLOCKS = NC * NX * NY
CHUNK = 512


def pieces():
    for zl in range(2):
        for y in range(NY):
            for a in range(NX // 2):
                src = []
                for j in range(4):
                    block = ((j & 1) * NX + 2 * a + (j >> 1)) * NY + y
                    src.append(block * SPAN + ROWS * zl)
                yield 2 * GROUP * NY * zl + 2 * GROUP * y + GROUP * a, src


STEP_ROWS = 2 * 2 * GROUP * NY


def fold(v):
    total = v[:, :LANES]
    for i in range(1, v.shape[1] // LANES):
        total = total + v[:, i * LANES : (i + 1) * LANES]
    return total


def squares_kernel(tok_ref, out_ref):
    total = jnp.zeros(out_ref.shape, jnp.float32)
    for i in range(0, tok_ref.shape[1], CHUNK):
        x = tok_ref[:, i : i + CHUNK].astype(jnp.float32)
        total = total + fold(x * x)
    out_ref[...] = total


def finish_kernel(tok_ref, wb_ref, gain_ref, cot_ref, stat_ref, out_ref):
    inverse, mean = stat_ref[0, :, :1], stat_ref[1, :, :1]
    per = CHUNK // LANES
    for k in range(tok_ref.shape[1] // CHUNK):
        at = slice(k * CHUNK, (k + 1) * CHUNK)
        hidden_grad = lax.dot_general(
            cot_ref[...], wb_ref[at, :], (((1,), (1,)), ((), ())), preferred_element_type=jnp.float32
        )
        gain = jnp.concatenate([gain_ref[k * per + n : k * per + n + 1, :] for n in range(per)], axis=1)
        normed = tok_ref[:, at].astype(jnp.float32) * inverse
        out_ref[:, at] = (inverse * (hidden_grad * gain - normed * mean)).astype(out_ref.dtype)


def kernel(
    tok_ref, own_ref, oth_ref, cot_ref, sq_ref,
    val_ref, wb_ref, gain_ref, stat_ref, keep_ref, send_ref,
    w_ref, st_ref, p_ref,
):
    rows, width = tok_ref.shape
    gain_rows = width // LANES
    zone = NZ * ROWS
    mine = core()
    half = BLOCKS // 2 * SPAN

    def region(stage, core_at):
        return stage.at[pl.ds(pl.multiple_of(core_at * half, half), half)]

    for zz in range(STEPS):
        stage = st_ref.at[zz % 2]
        for core_at, ref in ((mine, own_ref), (1 - mine, oth_ref)):
            to = region(stage, core_at)
            for s in range(BLOCKS // 2):
                start = s * zone + zz * SPAN
                to[s * SPAN : (s + 1) * SPAN, :] = ref[start : start + SPAN, :].astype(jnp.float32)
        for base, src in pieces():
            base = base + zz * STEP_ROWS
            for j in range(4):
                lo = 0 if j == 0 else 1
                t = src[j]
                w_ref[base + OFFS[j] + lo : base + OFFS[j] + lo + 10, :] = stage[t + lo : t + lo + 10, :]
                if j < 3:
                    at = 10 if j == 0 else 11
                    w_ref[base + OFFS[j + 1] : base + OFFS[j + 1] + 1, :] = (
                        stage[t + at : t + at + 1, :] + stage[src[j + 1] : src[j + 1] + 1, :]
                    )

    def cols(k):
        return pl.ds(pl.multiple_of(k * CHUNK, CHUNK), CHUNK)

    steps = width // CHUNK
    zero = jnp.zeros((rows, LANES), jnp.float32)
    inverse = lax.rsqrt(jnp.sum(sq_ref[...], axis=1, keepdims=True) * (1.0 / width) + 1e-05)
    per = CHUNK // LANES
    cot = cot_ref[...]
    p_ref[gain_rows + width :, :] = jnp.zeros((8, LANES), jnp.float32)

    def main(k, carry):
        values, dots = carry
        normed = tok_ref[:, cols(k)].astype(jnp.float32) * inverse
        gain = jnp.concatenate([w_ref[pl.ds(k * per + i, 1), :] for i in range(per)], axis=1)
        at = pl.ds(pl.multiple_of(gain_rows + k * CHUNK, 8), CHUNK)
        weight = w_ref[at, :].astype(jnp.bfloat16)
        wb_ref[pl.ds(pl.multiple_of(k * CHUNK, CHUNK), CHUNK), :] = weight
        hidden = (normed * gain).astype(jnp.bfloat16)
        values = values + jnp.dot(hidden, weight, preferred_element_type=jnp.float32)
        p_ref[at, :] = lax.dot_general(
            hidden, cot, (((0,), (0,)), ((), ())), preferred_element_type=jnp.float32
        )
        hidden_grad = lax.dot_general(
            cot, weight, (((1,), (1,)), ((), ())), preferred_element_type=jnp.float32
        )
        gain_grad = jnp.sum(hidden_grad * normed, axis=0, keepdims=True)
        for i in range(per):
            p_ref[pl.ds(k * per + i, 1), :] = gain_grad[:, i * LANES : (i + 1) * LANES]
        return values, dots + fold(hidden_grad * gain * normed)

    values, dots = lax.fori_loop(0, steps, main, (zero, zero), unroll=True)
    val_ref[...] = values.astype(val_ref.dtype)
    mean = jnp.sum(dots, axis=1, keepdims=True) * (1.0 / width)

    gain_ref[...] = w_ref[:gain_rows, :]
    stat_ref[0, :, :] = jnp.broadcast_to(inverse, (rows, LANES))
    stat_ref[1, :, :] = jnp.broadcast_to(mean, (rows, LANES))

    for zz in range(STEPS):
        stage = st_ref.at[zz % 2]
        for base, dst in pieces():
            for j in range(4):
                r = base + zz * STEP_ROWS + OFFS[j]
                stage[dst[j] : dst[j] + ROWS, :] = p_ref[r : r + ROWS, :]
        for core_at, ref in ((mine, keep_ref), (1 - mine, send_ref)):
            of = region(stage, core_at)
            for s in range(BLOCKS // 2):
                start = s * zone + zz * SPAN
                ref[start : start + SPAN, :] = of[s * SPAN : (s + 1) * SPAN, :].astype(ref.dtype)


def core():
    return lax.axis_index("c")


def call(body, outs, scratch, mib, flops, *args):
    vmem = pl.BlockSpec(memory_space=pltpu.VMEM)
    moved = sum(a.size * a.dtype.itemsize for a in (*args, *outs))
    return pl.pallas_call(
        body,
        out_shape=outs,
        in_specs=[vmem] * len(args),
        out_specs=tuple([vmem] * len(outs)),
        scratch_shapes=scratch,
        compiler_params=pltpu.CompilerParams(vmem_limit_bytes=mib * 1024 * 1024),
        cost_estimate=pl.CostEstimate(flops=flops, bytes_accessed=moved, transcendentals=0),
    )(*args)


def squares(tokens):
    rows, _ = tokens.shape
    outs = (jax.ShapeDtypeStruct((rows, LANES), jnp.float32),)
    return call(squares_kernel, outs, [], 8, 2 * tokens.size, tokens)[0]


def finish(tokens, weight, gain, cotangent, stats):
    outs = (jax.ShapeDtypeStruct(tokens.shape, tokens.dtype),)
    flops = 2 * tokens.size * LANES
    return call(finish_kernel, outs, [], 12, flops, tokens, weight, gain, cotangent, stats)[0]


def local_step(tokens, own, other, cotangent, squared):
    rows, width = tokens.shape
    total = width // LANES + width
    outs = (
        jax.ShapeDtypeStruct(cotangent.shape, jnp.bfloat16),
        jax.ShapeDtypeStruct((width, LANES), jnp.bfloat16),
        jax.ShapeDtypeStruct((width // LANES, LANES), jnp.float32),
        jax.ShapeDtypeStruct((2, rows, LANES), jnp.float32),
        jax.ShapeDtypeStruct(own.shape, jnp.bfloat16),
        jax.ShapeDtypeStruct(own.shape, jnp.bfloat16),
    )
    scratch = [
        pltpu.VMEM((total, LANES), jnp.float32),
        pltpu.VMEM((2, BLOCKS * SPAN, LANES), jnp.float32),
        pltpu.VMEM((total + 8, LANES), jnp.float32),
    ]
    flops = 6 * tokens.size * LANES
    return call(kernel, outs, scratch, 24, flops, tokens, own, other, cotangent, squared)


def spread(piece, axis, count):
    return lax.all_to_all(
        jnp.broadcast_to(piece[None], (count,) + piece.shape), axis, 0, 0, tiled=True
    )


def collect(parts, axis, dtype):
    got = lax.all_to_all(parts.astype(dtype), axis, 0, 0, tiled=True)
    return jnp.sum(got.astype(jnp.float32), axis=0)


def swap(half):
    return lax.ppermute(half, "c", ((0, 1), (1, 0)))


def phase():
    j = (lax.axis_index("x") % 2) * 2 + lax.axis_index("c")
    return (j * 96) % LANES


def program(tokens, flat_params, cotangent):
    shard_len = flat_params.shape[0]
    offset = phase()
    piece = lax.dynamic_update_slice(
        jnp.zeros((ROWS * LANES,), flat_params.dtype), flat_params, (offset,)
    ).reshape(ROWS, LANES)
    piece = spread(piece, "z", NZ).reshape(NZ * ROWS, LANES)
    piece = spread(piece, Y, NY).reshape(NY * NZ * ROWS, LANES)
    piece = spread(piece, "x", NX).reshape(NX * NY * NZ * ROWS, LANES)
    other = swap(piece)
    values, weight, gain, stats, kept, sent = local_step(
        tokens, piece, other, cotangent, squares(tokens)
    )
    token_grads = finish(tokens, weight, gain, cotangent, stats)
    grads = kept.astype(jnp.float32) + swap(sent).astype(jnp.float32)
    grads = collect(grads.reshape(NX, -1, LANES), "x", jnp.bfloat16)
    grads = collect(grads.reshape(NY, -1, LANES), Y, jnp.bfloat16)
    grads = collect(grads.reshape(NZ, ROWS, LANES), "z", jnp.float32)
    owned = lax.dynamic_slice(grads.reshape(-1), (offset,), (shard_len,))
    return values, token_grads, owned


def solution(mesh):
    split = Mesh(mesh.devices.reshape(NZ, NYH, NYL, NX, NC), ALL)
    specs = (P(ALL, None), P(ALL), P(ALL, None))
    return jax.shard_map(
        program,
        mesh=split,
        in_specs=specs,
        out_specs=(P(ALL, None), P(ALL, None), P(ALL)),
        check_vma=False,
    )
```

```python
import jax
import jax.numpy as jnp
from jax import lax
from jax.experimental import pallas as pl
from jax.experimental.pallas import tpu as pltpu
from jax.sharding import Mesh, PartitionSpec as P

NZ, NYH, NYL, NX, NC = 12, 2, 4, 4, 2
NY = NYH * NYL
Y = ("yh", "yl")
ALL = ("z", "yh", "yl", "x", "c")
LANES = 128
ROWS = 12
GROUP = 43
OFFS = (0, 10, 21, 32)
SPAN = 24
STEPS = NZ // 2
BLOCKS = NC * NX * NY
CHUNK = 512


def pieces():
    for zl in range(2):
        for y in range(NY):
            for a in range(NX // 2):
                src = []
                for j in range(4):
                    block = ((j & 1) * NX + 2 * a + (j >> 1)) * NY + y
                    src.append(block * SPAN + ROWS * zl)
                yield 2 * GROUP * NY * zl + 2 * GROUP * y + GROUP * a, src


STEP_ROWS = 2 * 2 * GROUP * NY


def fold(v):
    total = v[:, :LANES]
    for i in range(1, v.shape[1] // LANES):
        total = total + v[:, i * LANES : (i + 1) * LANES]
    return total


def squares_kernel(tok_ref, out_ref):
    total = jnp.zeros(out_ref.shape, jnp.float32)
    for i in range(0, tok_ref.shape[1], CHUNK):
        x = tok_ref[:, i : i + CHUNK].astype(jnp.float32)
        total = total + fold(x * x)
    out_ref[...] = total


def finish_kernel(tok_ref, wb_ref, gain_ref, cot_ref, stat_ref, out_ref):
    inverse, mean = stat_ref[0, :, :1], stat_ref[1, :, :1]
    per = CHUNK // LANES
    for k in range(tok_ref.shape[1] // CHUNK):
        at = slice(k * CHUNK, (k + 1) * CHUNK)
        hidden_grad = lax.dot_general(
            cot_ref[...], wb_ref[at, :], (((1,), (1,)), ((), ())), preferred_element_type=jnp.float32
        )
        gain = jnp.concatenate([gain_ref[k * per + n : k * per + n + 1, :] for n in range(per)], axis=1)
        normed = tok_ref[:, at].astype(jnp.float32) * inverse
        out_ref[:, at] = (inverse * (hidden_grad * gain - normed * mean)).astype(out_ref.dtype)


def kernel(
    tok_ref, own_ref, oth_ref, cot_ref, sq_ref,
    val_ref, wb_ref, gain_ref, stat_ref, keep_ref, send_ref,
    w_ref, st0_ref, st1_ref, p_ref,
):
    rows, width = tok_ref.shape
    gain_rows = width // LANES
    zone = NZ * ROWS
    mine = core()
    half = BLOCKS // 2 * SPAN

    def region(stage, core_at):
        return stage.at[pl.ds(pl.multiple_of(core_at * half, half), half)]

    for zz in range(STEPS):
        stage = (st0_ref, st1_ref)[zz % 2]
        for core_at, ref in ((mine, own_ref), (1 - mine, oth_ref)):
            to = region(stage, core_at)
            for s in range(BLOCKS // 2):
                start = s * zone + zz * SPAN
                to[s * SPAN : (s + 1) * SPAN, :] = ref[start : start + SPAN, :].astype(jnp.float32)
        for base, src in pieces():
            base = base + zz * STEP_ROWS
            for j in range(4):
                lo = 0 if j == 0 else 1
                t = src[j]
                w_ref[base + OFFS[j] + lo : base + OFFS[j] + lo + 10, :] = stage[t + lo : t + lo + 10, :]
                if j < 3:
                    at = 10 if j == 0 else 11
                    w_ref[base + OFFS[j + 1] : base + OFFS[j + 1] + 1, :] = (
                        stage[t + at : t + at + 1, :] + stage[src[j + 1] : src[j + 1] + 1, :]
                    )

    def cols(k):
        return pl.ds(pl.multiple_of(k * CHUNK, CHUNK), CHUNK)

    steps = width // CHUNK
    zero = jnp.zeros((rows, LANES), jnp.float32)
    inverse = lax.rsqrt(jnp.sum(sq_ref[...], axis=1, keepdims=True) * (1.0 / width) + 1e-05)
    per = CHUNK // LANES
    cot = cot_ref[...]
    p_ref[gain_rows + width :, :] = jnp.zeros((8, LANES), jnp.float32)

    def main(k, carry):
        values, dots = carry
        normed = tok_ref[:, cols(k)].astype(jnp.float32) * inverse
        gain = jnp.concatenate([w_ref[pl.ds(k * per + i, 1), :] for i in range(per)], axis=1)
        at = pl.ds(pl.multiple_of(gain_rows + k * CHUNK, 8), CHUNK)
        weight = w_ref[at, :].astype(jnp.bfloat16)
        wb_ref[pl.ds(pl.multiple_of(k * CHUNK, CHUNK), CHUNK), :] = weight
        hidden = (normed * gain).astype(jnp.bfloat16)
        values = values + jnp.dot(hidden, weight, preferred_element_type=jnp.float32)
        p_ref[at, :] = lax.dot_general(
            hidden, cot, (((0,), (0,)), ((), ())), preferred_element_type=jnp.float32
        )
        hidden_grad = lax.dot_general(
            cot, weight, (((1,), (1,)), ((), ())), preferred_element_type=jnp.float32
        )
        gain_grad = jnp.sum(hidden_grad * normed, axis=0, keepdims=True)
        for i in range(per):
            p_ref[pl.ds(k * per + i, 1), :] = gain_grad[:, i * LANES : (i + 1) * LANES]
        return values, dots + fold(hidden_grad * gain * normed)

    values, dots = lax.fori_loop(0, steps, main, (zero, zero), unroll=True)
    val_ref[...] = values.astype(val_ref.dtype)
    mean = jnp.sum(dots, axis=1, keepdims=True) * (1.0 / width)

    gain_ref[...] = w_ref[:gain_rows, :]
    stat_ref[0, :, :] = jnp.broadcast_to(inverse, (rows, LANES))
    stat_ref[1, :, :] = jnp.broadcast_to(mean, (rows, LANES))

    for zz in range(STEPS):
        stage = (st0_ref, st1_ref)[zz % 2]
        for base, dst in pieces():
            for j in range(4):
                r = base + zz * STEP_ROWS + OFFS[j]
                stage[dst[j] : dst[j] + ROWS, :] = p_ref[r : r + ROWS, :]
        for core_at, ref in ((mine, keep_ref), (1 - mine, send_ref)):
            of = region(stage, core_at)
            for s in range(BLOCKS // 2):
                start = s * zone + zz * SPAN
                ref[start : start + SPAN, :] = of[s * SPAN : (s + 1) * SPAN, :].astype(ref.dtype)


def core():
    return lax.axis_index("c")


def call(body, outs, scratch, mib, flops, *args):
    vmem = pl.BlockSpec(memory_space=pltpu.VMEM)
    moved = sum(a.size * a.dtype.itemsize for a in (*args, *outs))
    return pl.pallas_call(
        body,
        out_shape=outs,
        in_specs=[vmem] * len(args),
        out_specs=tuple([vmem] * len(outs)),
        scratch_shapes=scratch,
        compiler_params=pltpu.CompilerParams(vmem_limit_bytes=mib * 1024 * 1024),
        cost_estimate=pl.CostEstimate(flops=flops, bytes_accessed=moved, transcendentals=0),
    )(*args)


def squares(tokens):
    rows, _ = tokens.shape
    outs = (jax.ShapeDtypeStruct((rows, LANES), jnp.float32),)
    return call(squares_kernel, outs, [], 8, 2 * tokens.size, tokens)[0]


def finish(tokens, weight, gain, cotangent, stats):
    outs = (jax.ShapeDtypeStruct(tokens.shape, tokens.dtype),)
    flops = 2 * tokens.size * LANES
    return call(finish_kernel, outs, [], 12, flops, tokens, weight, gain, cotangent, stats)[0]


def local_step(tokens, own, other, cotangent, squared):
    rows, width = tokens.shape
    total = width // LANES + width
    outs = (
        jax.ShapeDtypeStruct(cotangent.shape, jnp.bfloat16),
        jax.ShapeDtypeStruct((width, LANES), jnp.bfloat16),
        jax.ShapeDtypeStruct((width // LANES, LANES), jnp.float32),
        jax.ShapeDtypeStruct((2, rows, LANES), jnp.float32),
        jax.ShapeDtypeStruct(own.shape, jnp.bfloat16),
        jax.ShapeDtypeStruct(own.shape, jnp.bfloat16),
    )
    scratch = [
        pltpu.VMEM((total, LANES), jnp.float32),
        pltpu.VMEM((BLOCKS * SPAN, LANES), jnp.float32),
        pltpu.VMEM((BLOCKS * SPAN, LANES), jnp.float32),
        pltpu.VMEM((total + 8, LANES), jnp.float32),
    ]
    flops = 6 * tokens.size * LANES
    return call(kernel, outs, scratch, 24, flops, tokens, own, other, cotangent, squared)


def spread(piece, axis, count):
    return lax.all_to_all(
        jnp.broadcast_to(piece[None], (count,) + piece.shape), axis, 0, 0, tiled=True
    )


def collect(parts, axis, dtype):
    got = lax.all_to_all(parts.astype(dtype), axis, 0, 0, tiled=True)
    return jnp.sum(got.astype(jnp.float32), axis=0)


def swap(half):
    return lax.ppermute(half, "c", ((0, 1), (1, 0)))


def phase():
    j = (lax.axis_index("x") % 2) * 2 + lax.axis_index("c")
    return (j * 96) % LANES


def program(tokens, flat_params, cotangent):
    shard_len = flat_params.shape[0]
    offset = phase()
    piece = lax.dynamic_update_slice(
        jnp.zeros((ROWS * LANES,), flat_params.dtype), flat_params, (offset,)
    ).reshape(ROWS, LANES)
    piece = spread(piece, "z", NZ).reshape(NZ * ROWS, LANES)
    piece = spread(piece, Y, NY).reshape(NY * NZ * ROWS, LANES)
    piece = spread(piece, "x", NX).reshape(NX * NY * NZ * ROWS, LANES)
    other = swap(piece)
    values, weight, gain, stats, kept, sent = local_step(
        tokens, piece, other, cotangent, squares(tokens)
    )
    token_grads = finish(tokens, weight, gain, cotangent, stats)
    grads = kept.astype(jnp.float32) + swap(sent).astype(jnp.float32)
    grads = collect(grads.reshape(NX, -1, LANES), "x", jnp.bfloat16)
    grads = collect(grads.reshape(NY, -1, LANES), Y, jnp.bfloat16)
    grads = collect(grads.reshape(NZ, ROWS, LANES), "z", jnp.bfloat16)
    owned = lax.dynamic_slice(grads.reshape(-1), (offset,), (shard_len,))
    return values, token_grads, owned


def solution(mesh):
    split = Mesh(mesh.devices.reshape(NZ, NYH, NYL, NX, NC), ALL)
    specs = (P(ALL, None), P(ALL), P(ALL, None))
    return jax.shard_map(
        program,
        mesh=split,
        in_specs=specs,
        out_specs=(P(ALL, None), P(ALL, None), P(ALL)),
        check_vma=False,
    )
```
